512 devices in a mesh: slab: 128 (over z, y, core), mirror: 4 (over x).
Axes of the slice: x: 4, y: 4, z: 16, core: 2. Of those that a mesh axis runs over, the one named last changes fastest.
Arguments:
- a_blocks: bfloat16 [16384, 7, 4096], P(('slab', 'mirror'))
- a_cols: int32 [16384, 7], P(('slab', 'mirror')), may hold values from 0 to 16383, as said below
- p_blocks: bfloat16 [16384, 4096], P(('slab', 'mirror'))
- p_agg: int32 [16384], P(('slab', 'mirror')), may hold values from 0 to 8191, as said below
Outputs:
- coarse_blocks: bfloat16 [8192, 7, 4096], P(('slab', 'mirror'))
- jacobi_inverses: float32 [8192, 4096], P(('slab', 'mirror'))
The draws below stay inside these ranges and needn't reach their ends.
Inputs may be any that keep to these rules, and one draw needn't show every extreme that they name: `a_cols`: block 0 of row g has column g. Every other column of a row on the device of flattened index s * 4 + m lies on a device of the same slab index and mirror index m - 1, m or m + 1, each device holding 32 consecutive rows. The two fine rows of one aggregate have their k-th columns in one common aggregate. `p_agg`: each aggregate holds exactly two fine rows, at the same mirror index on the two devices whose slab indices differ in the lowest bit; aggregate c belongs to the device of flattened index c // 16, which is one of those two, and each of the two devices owns half of the pair's aggregates.
All inputs are finite; a program needn't handle non-finite values.
Results may differ from the reference program's by a relative error of at most 0.0075.
Values may be sent and summed in bfloat16 or wider, within the bound.
A program may use at most 64 MiB of HBM per device.

```python
import jax
import jax.numpy as jnp
from jax import lax

BLOCK = 64
KA = 7
BR_DEV = 32
NB = 16384
N_SLAB = 128
N_MIRROR = 4


def build_maps(key):
    rows = BR_DEV
    mirrors = N_MIRROR
    groups = N_SLAB // 2
    keyperm, keydelta, keypick = jax.random.split(jax.random.fold_in(key, 7), 3)
    pkeys = jax.random.split(keyperm, groups * mirrors)
    perm = jax.vmap(lambda one: jax.random.permutation(one, rows))(pkeys).reshape(groups, mirrors, rows).astype(jnp.int32)
    delta = jax.random.randint(keydelta, (groups, mirrors, rows, KA - 1), -1, 2).astype(jnp.int32)
    mirror4 = jnp.arange(mirrors, dtype=jnp.int32)[None, :, None, None]
    target = jnp.clip(mirror4 + delta, 0, mirrors - 1)
    picked = jax.random.randint(keypick, (groups, mirrors, rows, KA - 1), 0, rows).astype(jnp.int32)
    group4 = jnp.arange(groups, dtype=jnp.int32)[:, None, None, None]
    col_even = (2 * group4 * mirrors + target) * rows + picked
    col_odd = ((2 * group4 + 1) * mirrors + target) * rows + perm[group4, target, picked]
    group3 = jnp.arange(groups, dtype=jnp.int32)[:, None, None]
    mirror3 = jnp.arange(mirrors, dtype=jnp.int32)[None, :, None]
    local = jnp.broadcast_to(jnp.arange(rows, dtype=jnp.int32)[None, None, :], (groups, mirrors, rows))
    own_even = (2 * group3 * mirrors + mirror3) * rows + local
    own_odd = ((2 * group3 + 1) * mirrors + mirror3) * rows + perm
    cols_even = jnp.concatenate([own_even[..., None], col_even], axis=-1)
    paired = jnp.concatenate([own_odd[..., None], col_odd], axis=-1)
    cols_odd = jnp.zeros_like(cols_even).at[group3, mirror3, perm].set(paired)
    cols = jnp.stack([cols_even, cols_odd], axis=1).reshape(NB, KA)
    half = rows // 2
    parity = local // half
    coarse_even = ((2 * group3 + parity) * mirrors + mirror3) * half + local % half
    coarse_odd = jnp.zeros_like(coarse_even).at[group3, mirror3, perm].set(coarse_even)
    agg = jnp.stack([coarse_even, coarse_odd], axis=1).reshape(NB)
    return (cols.astype(jnp.int32), agg.astype(jnp.int32))


def draw_a_cols(key, part):
    return build_maps(key)[0]


def draw_p_agg(key, part):
    return build_maps(key)[1]


def identity_flat():
    index = jnp.arange(BLOCK * BLOCK, dtype=jnp.int32)
    return (index // BLOCK == index % BLOCK).astype(jnp.float32)


def draw_a_blocks(key, part):
    shape = (NB, KA, BLOCK * BLOCK)
    noise = jax.random.truncated_normal(key, -3.0, 3.0, shape, jnp.float32)
    values = noise * (0.5 / BLOCK ** 0.5)
    slot_zero = (jnp.arange(KA, dtype=jnp.int32) == 0).astype(jnp.float32)
    values = values + 4.0 * slot_zero[None, :, None] * identity_flat()[None, None, :]
    return values.astype(jnp.bfloat16)


def draw_p_blocks(key, part):
    shape = (NB, BLOCK * BLOCK)
    noise = jax.random.truncated_normal(key, -3.0, 3.0, shape, jnp.float32)
    values = noise * (0.25 / BLOCK ** 0.5) + identity_flat()[None, :]
    return values.astype(jnp.bfloat16)


def setup_inputs(seed: int = 0) -> dict:
    arg_keys = jax.random.split(jax.random.key(seed), 5)
    a_blocks = draw_a_blocks(jax.random.fold_in(arg_keys[4], 71), 0)
    a_cols = draw_a_cols(jax.random.fold_in(arg_keys[4], 71), 0)
    p_blocks = draw_p_blocks(jax.random.fold_in(arg_keys[4], 71), 0)
    p_agg = draw_p_agg(jax.random.fold_in(arg_keys[4], 71), 0)
    return dict(a_blocks=a_blocks, a_cols=a_cols, p_blocks=p_blocks, p_agg=p_agg)


def invert_block(matrix):
    lower = jnp.linalg.cholesky(matrix)
    ident = jnp.eye(matrix.shape[0], dtype=matrix.dtype)
    return jax.scipy.linalg.cho_solve((lower, True), ident)

def reference(a_blocks, a_cols, p_blocks, p_agg):
    nfine = a_blocks.shape[0]
    ncoarse = nfine // 2
    kblk = a_blocks.shape[1]
    rows = BR_DEV
    total0 = jnp.zeros((ncoarse, kblk, BLOCK, BLOCK), jnp.float32)

    def advance(index, total):
        start = (index * rows).astype(jnp.int32)
        blocks = lax.dynamic_slice_in_dim(a_blocks, start, rows, 0).reshape(rows, kblk, BLOCK, BLOCK)
        columns = lax.dynamic_slice_in_dim(a_cols, start, rows, 0)
        targets = lax.dynamic_slice_in_dim(p_agg, start, rows, 0)
        own = lax.dynamic_slice_in_dim(p_blocks, start, rows, 0).reshape(rows, BLOCK, BLOCK)
        remote = jnp.take(p_blocks, columns.reshape(-1), axis=0).reshape(rows, kblk, BLOCK, BLOCK)
        product = jnp.einsum('rkij,rkjl->rkil', blocks.astype(jnp.float32), remote.astype(jnp.float32)).astype(jnp.bfloat16)
        term = jnp.einsum('rji,rkjl->rkil', own.astype(jnp.float32), product.astype(jnp.float32))
        return total.at[targets].add(term)
    total = lax.fori_loop(0, nfine // rows, advance, total0)
    coarse_blocks = total.reshape(ncoarse, kblk, BLOCK * BLOCK).astype(jnp.bfloat16)
    diagonal = total[:, 0]
    symmetric = 0.5 * (diagonal + jnp.swapaxes(diagonal, 1, 2))
    jacobi_inverses = jax.vmap(invert_block)(symmetric).reshape(ncoarse, BLOCK * BLOCK)
    return (coarse_blocks, jacobi_inverses)
```

```python
import jax
import jax.numpy as jnp
from jax import lax
from jax.experimental import pallas as pl
from jax.experimental.pallas import tpu as pltpu
from jax.sharding import PartitionSpec as P

F32, BF16 = jnp.float32, jnp.bfloat16
BLOCK = 64
LANES = 128
ROWS = 32
HALF = ROWS // 2
PAIRS = HALF // 2
KA = 7
TILES = BLOCK * BLOCK // LANES
CHUNKS = 4
MESH = pl.DeviceIdType.MESH


def rotate(value):
    return pltpu.roll(value, BLOCK, 1)


def dot(left, right):
    return lax.dot_general(left, right, (((1,), (0,)), ((), ())), preferred_element_type=F32)


def rows_of(index, count):
    return pl.ds(pl.multiple_of(index * count, count), count)


def blocks_from_rows(flat, blocks, at):
    blocks = blocks.reshape(blocks.shape[0] * TILES, LANES)
    for t in range(TILES):
        tile = flat[:, t * LANES:(t + 1) * LANES].astype(F32)
        blocks[pl.ds(at * TILES + t, ROWS, stride=TILES), :] = tile


def tiles_from_rows(flat, left_tiles, right_tiles, at):
    left = lax.broadcasted_iota(jnp.int32, (ROWS, LANES), 1) < BLOCK
    left_tiles = left_tiles.reshape(left_tiles.shape[0] * BLOCK, LANES)
    right_tiles = right_tiles.reshape(right_tiles.shape[0] * BLOCK, LANES)
    for t in range(TILES):
        tile = flat[:, t * LANES:(t + 1) * LANES].astype(F32)
        turned = rotate(tile)
        even = pl.ds(at * BLOCK + 2 * t, ROWS, stride=BLOCK)
        odd = pl.ds(at * BLOCK + 2 * t + 1, ROWS, stride=BLOCK)
        left_tiles[even, :] = jnp.where(left, tile, 0.0)
        left_tiles[odd, :] = jnp.where(left, turned, 0.0)
        right_tiles[even, :] = jnp.where(left, 0.0, turned)
        right_tiles[odd, :] = jnp.where(left, 0.0, tile)


def transposed_tiles(left_tiles, flipped):
    r = lax.broadcasted_iota(jnp.int32, (BLOCK, LANES), 0)
    c = lax.broadcasted_iota(jnp.int32, (BLOCK, LANES), 1)
    pick = (c == 2 * (r % 32) + r // 32).astype(BF16)
    wide = c < BLOCK
    left_tiles = left_tiles.reshape(left_tiles.shape[0] * BLOCK, LANES)

    def body(p, carry):
        parts = []
        for side in range(2):
            start = pl.multiple_of((ROWS + 2 * p + side) * BLOCK, BLOCK)
            parts.append(left_tiles[pl.ds(start, 32, stride=2), :])
            parts.append(left_tiles[pl.ds(start + 1, 32, stride=2), :])
        stacked = jnp.concatenate(parts, axis=0).astype(BF16)
        both = lax.dot_general(pick, stacked, (((1,), (1,)), ((), ())), preferred_element_type=F32)
        turned = rotate(both)
        flipped[2 * p] = jnp.where(wide, both, turned).astype(BF16)
        flipped[2 * p + 1] = jnp.where(wide, turned, both).astype(BF16)
        return carry

    lax.fori_loop(0, HALF, body, 0)


def pair_flipped(p, table, flipped):
    wide = lax.broadcasted_iota(jnp.int32, (BLOCK, LANES), 1) < BLOCK
    one = flipped[table[(2 * p) * 8 + KA]]
    two = flipped[table[(2 * p + 1) * 8 + KA]]
    return jnp.where(wide, one, two)


def pair_terms(p, k, outer, table, blocks, left_tiles, right_tiles):
    left = lax.broadcasted_iota(jnp.int32, (32, LANES), 1) < BLOCK
    wide = lax.broadcasted_iota(jnp.int32, (BLOCK, LANES), 1) < BLOCK
    first, second = 2 * p, 2 * p + 1
    a1 = blocks[k * ROWS + table[first * 8 + KA]]
    a2 = blocks[k * ROWS + table[second * 8 + KA]]
    even = jnp.where(left, a1, rotate(a2))
    odd = jnp.where(left, rotate(a1), a2)
    lhs = jnp.concatenate([even, odd], axis=0).astype(BF16)
    rhs = jnp.concatenate(
        [
            left_tiles[table[first * 8 + k]],
            right_tiles[table[second * 8 + k]],
        ],
        axis=0,
    ).astype(BF16)
    product = dot(lhs, rhs)
    spread = jnp.concatenate(
        [jnp.where(wide, product, 0.0), jnp.where(wide, 0.0, product)], axis=0
    ).astype(BF16)
    return dot(outer, spread)


def split_pair(total):
    left = lax.broadcasted_iota(jnp.int32, (32, LANES), 1) < BLOCK
    even, odd = total[:32], total[32:]
    return jnp.where(left, even, rotate(odd)), jnp.where(left, rotate(even), odd)


def invert_all(v):
    lanes = lax.broadcasted_iota(jnp.int32, (BLOCK, LANES), 1)
    sub = lax.broadcasted_iota(jnp.int32, (BLOCK, LANES), 0)

    def body(tk, carry):
        for inner in range(16):
            h, q = inner % 2, inner // 2
            k = tk * 16 + inner
            index = (lanes // 8) * 8 + q
            slabs = [(2 * tk + h + d) % 8 for d in range(8)]
            cols = [v[pl.ds(s * BLOCK + k, 1), :] for s in slabs]
            row = jnp.take_along_axis(v[rows_of(slabs[0], BLOCK), :], index, axis=1)
            pivot = jnp.take_along_axis(
                jnp.broadcast_to(cols[0], (8, LANES)), index[:8], axis=1
            )[:1]
            inverse = 1.0 / pivot
            here = sub == k
            scaled = jnp.where(here, inverse, row * inverse)
            for d in range(8):
                slab = v[rows_of(slabs[d], BLOCK), :]
                new = jnp.where(here, 0.0, slab) - cols[d] * scaled
                if d == 0:
                    new = jnp.where(lanes % 8 == q, scaled, new)
                v[rows_of(slabs[d], BLOCK), :] = new
        return carry

    lax.fori_loop(0, 4, body, 0)


def kernel(
    table, a_hbm, p_hbm, coarse_ref, inverse_ref,
    a_flat, p_flat, halo, blocks, left_tiles, right_tiles, flipped,
    first_send, first_got, rest_send, rest_got, kept, whole, nat, v,
    a_sem, p_sem, halo_send, halo_recv, first_sem, rest_send_sem, rest_recv_sem,
):
    slab = lax.axis_index("slab")
    mirror = lax.axis_index("mirror")
    mirrors = lax.axis_size("mirror")
    partner = slab + 1 - 2 * (slab % 2)
    up = (mirror + 1) % mirrors
    down = (mirror + mirrors - 1) % mirrors
    others = ({"mirror": up}, {"mirror": down}, {"slab": partner})

    own = pltpu.make_async_copy(p_hbm, p_flat, p_sem)
    own.start()
    loads = [
        pltpu.make_async_copy(a_hbm.at[k], a_flat.at[k], a_sem.at[k]) for k in range(KA)
    ]
    for load in loads:
        load.start()

    barrier = pltpu.get_barrier_semaphore()
    for other in others:
        pl.semaphore_signal(barrier, inc=1, device_id=other, device_id_type=MESH)
    pl.semaphore_wait(barrier, 3)

    halos = [
        pltpu.make_async_remote_copy(
            src_ref=p_hbm, dst_ref=halo.at[side], send_sem=halo_send.at[side],
            recv_sem=halo_recv.at[side], device_id=target, device_id_type=MESH,
        )
        for side, target in enumerate(({"mirror": up}, {"mirror": down}))
    ]
    for copy in halos:
        copy.start()

    own.wait()
    tiles_from_rows(p_flat, left_tiles, right_tiles, ROWS)
    transposed_tiles(left_tiles, flipped)
    loads[0].wait()
    blocks_from_rows(a_flat.at[0], blocks, 0)

    args = (table, blocks, left_tiles, right_tiles)

    def first_out(p, carry):
        outer = pair_flipped(p, table, flipped)
        first_send[rows_of(p, BLOCK), :] = pair_terms(p, 0, outer, *args).astype(BF16)
        return carry

    lax.fori_loop(0, PAIRS, first_out, 0)
    first = pltpu.make_async_remote_copy(
        src_ref=first_send, dst_ref=first_got, send_sem=first_sem.at[0],
        recv_sem=first_sem.at[1], device_id={"slab": partner}, device_id_type=MESH,
    )
    first.start()

    def first_kept(p, carry):
        outer = pair_flipped(p + PAIRS, table, flipped)
        kept[rows_of(p, BLOCK), :] = pair_terms(p + PAIRS, 0, outer, *args)
        return carry

    lax.fori_loop(0, PAIRS, first_kept, 0)

    for k in range(1, KA):
        loads[k].wait()

    def rest_blocks(k, carry):
        blocks_from_rows(a_flat.at[k], blocks, k * ROWS)
        return carry

    lax.fori_loop(1, KA, rest_blocks, 0)

    first.wait()

    wide = lax.broadcasted_iota(jnp.int32, (BLOCK, LANES), 1) < BLOCK

    def diagonal(p, carry):
        total = kept[rows_of(p, BLOCK), :] + first_got[rows_of(p, BLOCK), :].astype(F32)
        one, two = split_pair(total)
        whole[rows_of(2 * p, TILES), :] = one
        whole[rows_of(2 * p + 1, TILES), :] = two
        at = pl.multiple_of(p * BLOCK, BLOCK)
        nat[pl.ds(at, 32, stride=2), :] = total[:32]
        nat[pl.ds(at + 1, 32, stride=2), :] = total[32:]
        plain = nat[rows_of(p, BLOCK), :]
        turned = jnp.concatenate([plain, plain], axis=0).T
        turned = jnp.where(wide, turned[:BLOCK], turned[BLOCK:])
        nat[rows_of(p, BLOCK), :] = 0.5 * (plain + turned)
        even = nat[pl.ds(at, 32, stride=2), :]
        odd = nat[pl.ds(at + 1, 32, stride=2), :]
        one, two = split_pair(jnp.concatenate([even, odd], axis=0))
        kept[rows_of(2 * p, TILES), :] = one
        kept[rows_of(2 * p + 1, TILES), :] = two
        return carry

    lax.fori_loop(0, PAIRS, diagonal, 0)
    for tk in range(4):
        stacked = jnp.concatenate(
            [kept[pl.ds(b * TILES + tk * 8, 8), :] for b in range(HALF)], axis=0
        )
        v[pl.ds(tk * LANES, LANES), :] = stacked.T
    invert_all(v)
    for tk in range(4):
        stacked = v[pl.ds(tk * LANES, LANES), :].T
        for b in range(HALF):
            nat[pl.ds(b * TILES + tk * 8, 8), :] = stacked[b * 8:(b + 1) * 8]
    for t in range(TILES):
        inverse_ref[:, t * LANES:(t + 1) * LANES] = nat[pl.ds(t, HALF, stride=TILES), :]

    for side in range(2):
        halos[side].wait()
        tiles_from_rows(halo.at[side], left_tiles, right_tiles, 2 * side * ROWS)

    per = PAIRS // CHUNKS
    sends = []
    for chunk in range(CHUNKS):
        def rest_out(p, carry):
            outer = pair_flipped(p, table, flipped)
            for k in range(1, KA):
                rest_send[p // per, rows_of((p % per) * (KA - 1) + k - 1, BLOCK), :] = (
                    pair_terms(p, k, outer, *args).astype(BF16)
                )
            return carry

        lax.fori_loop(chunk * per, (chunk + 1) * per, rest_out, 0)
        copy = pltpu.make_async_remote_copy(
            src_ref=rest_send.at[chunk], dst_ref=rest_got.at[chunk],
            send_sem=rest_send_sem.at[chunk], recv_sem=rest_recv_sem.at[chunk],
            device_id={"slab": partner}, device_id_type=MESH,
        )
        copy.start()
        sends.append(copy)

    def rest_kept(p, carry):
        outer = pair_flipped(p + PAIRS, table, flipped)
        for k in range(1, KA):
            kept[rows_of(p * (KA - 1) + k - 1, BLOCK), :] = pair_terms(p + PAIRS, k, outer, *args)
        return carry

    lax.fori_loop(0, PAIRS, rest_kept, 0)
    for chunk in range(CHUNKS):
        sends[chunk].wait()

        def add(p, carry):
            for k in range(1, KA):
                got = rest_got[p // per, rows_of((p % per) * (KA - 1) + k - 1, BLOCK), :]
                total = kept[rows_of(p * (KA - 1) + k - 1, BLOCK), :] + got.astype(F32)
                one, two = split_pair(total)
                whole[rows_of(k * HALF + 2 * p, TILES), :] = one
                whole[rows_of(k * HALF + 2 * p + 1, TILES), :] = two
            return carry

        lax.fori_loop(chunk * per, (chunk + 1) * per, add, 0)

    def flatten(k, carry):
        for t in range(TILES):
            tile = whole[pl.ds(k * HALF * TILES + t, HALF, stride=TILES), :]
            coarse_ref[k, :, t * LANES:(t + 1) * LANES] = tile.astype(BF16)
        return carry

    lax.fori_loop(0, KA, flatten, 0)


def on_device(a_blocks, a_cols, p_blocks, p_agg):
    mirrors = lax.axis_size("mirror")
    slab = lax.axis_index("slab")
    device = slab * mirrors + lax.axis_index("mirror")
    local = a_cols - (device - 1) * ROWS
    mine = ((p_agg // HALF) // mirrors) % 2 == slab % 2
    place = p_agg % HALF + HALF * mine.astype(jnp.int32)
    row = jnp.arange(ROWS, dtype=jnp.int32)
    full = jnp.concatenate([local, row[:, None]], axis=1)
    match = place[None, :] == row[:, None]
    table = jnp.sum(jnp.where(match[:, :, None], full[None], 0), axis=1).reshape(-1)

    vmem = lambda *shape: pltpu.VMEM(shape, F32)
    half = lambda *shape: pltpu.VMEM(shape, BF16)
    dma = pltpu.SemaphoreType.DMA
    coarse, inverse = pl.pallas_call(
        kernel,
        out_shape=(
            jax.ShapeDtypeStruct((KA, HALF, BLOCK * BLOCK), BF16),
            jax.ShapeDtypeStruct((HALF, BLOCK * BLOCK), F32),
        ),
        in_specs=[
            pl.BlockSpec(memory_space=pltpu.SMEM),
            pl.BlockSpec(memory_space=pl.ANY),
            pl.BlockSpec(memory_space=pl.ANY),
        ],
        out_specs=(
            pl.BlockSpec(memory_space=pltpu.VMEM),
            pl.BlockSpec(memory_space=pltpu.VMEM),
        ),
        scratch_shapes=[
            half(KA, ROWS, BLOCK * BLOCK),
            half(ROWS, BLOCK * BLOCK),
            half(2, ROWS, BLOCK * BLOCK),
            vmem(KA * ROWS, TILES, LANES),
            vmem(3 * ROWS, BLOCK, LANES),
            vmem(3 * ROWS, BLOCK, LANES),
            half(ROWS, BLOCK, LANES),
            half(PAIRS * BLOCK, LANES),
            half(PAIRS * BLOCK, LANES),
            half(CHUNKS, PAIRS // CHUNKS * (KA - 1) * BLOCK, LANES),
            half(CHUNKS, PAIRS // CHUNKS * (KA - 1) * BLOCK, LANES),
            vmem(PAIRS * (KA - 1) * BLOCK, LANES),
            vmem(KA * HALF * TILES, LANES),
            vmem(PAIRS * BLOCK, LANES),
            vmem(4 * LANES, LANES),
            dma((KA,)), dma, dma((2,)), dma((2,)), dma((2,)), dma((CHUNKS,)), dma((CHUNKS,)),
        ],
        compiler_params=pltpu.CompilerParams(
            collective_id=0, has_side_effects=True, vmem_limit_bytes=56 * 2**20
        ),
    )(table, jnp.transpose(a_blocks, (1, 0, 2)), p_blocks)
    return jnp.transpose(coarse, (1, 0, 2)), inverse


def solution(mesh):
    placed = (
        P(("slab", "mirror"), None, None),
        P(("slab", "mirror"), None),
        P(("slab", "mirror"), None),
        P(("slab", "mirror")),
    )
    return jax.shard_map(
        on_device,
        mesh=mesh,
        in_specs=placed,
        out_specs=(P(("slab", "mirror"), None, None), P(("slab", "mirror"), None)),
        check_vma=False,
    )
```

```python
import jax
import jax.numpy as jnp
from jax import lax
from jax.experimental import pallas as pl
from jax.experimental.pallas import tpu as pltpu
from jax.sharding import PartitionSpec as P

F32, BF16 = jnp.float32, jnp.bfloat16
BLOCK = 64
LANES = 128
ROWS = 32
HALF = ROWS // 2
PAIRS = HALF // 2
KA = 7
TILES = BLOCK * BLOCK // LANES
CHUNKS = 4
MESH = pl.DeviceIdType.MESH


def rotate(value):
    return pltpu.roll(value, BLOCK, 1)


def dot(left, right):
    return lax.dot_general(left, right, (((1,), (0,)), ((), ())), preferred_element_type=F32)


def rows_of(index, count):
    return pl.ds(pl.multiple_of(index * count, count), count)


def left_side(rows):
    return lax.broadcasted_iota(jnp.int32, (rows, LANES), 1) < BLOCK


def swap_matrix(swap):
    r = lax.broadcasted_iota(jnp.int32, (256, 256), 0)
    c = lax.broadcasted_iota(jnp.int32, (256, 256), 1)
    swap[...] = (c == (r % 16) * 16 + r // 16).astype(BF16)


def swapped(swap, parts):
    stacked = [jnp.concatenate(part, axis=0) for part in parts]
    return dot(swap[...], jnp.concatenate(stacked, axis=1)).astype(BF16)


def blocks_from_rows(tile, blocks, at, swap):
    for half in range(2):
        got = swapped(
            swap, [[tile(half, 16 * u + t) for t in range(16)] for u in range(2)]
        )
        for g in range(16):
            for u in range(2):
                blocks[at + 16 * half + g, 16 * u:16 * (u + 1), :] = (
                    got[16 * g:16 * (g + 1), u * LANES:(u + 1) * LANES]
                )


def tiles_from_rows(tile, tiles, at, swap):
    left = left_side(16)
    for half in range(2):
        for pair in range(2):
            parts = []
            for w in (2 * pair, 2 * pair + 1):
                part = []
                for t in range(8 * w, 8 * w + 8):
                    plain = tile(half, t)
                    turned = rotate(plain)
                    part += [jnp.where(left, plain, turned), jnp.where(left, turned, plain)]
                parts.append(part)
            got = swapped(swap, parts)
            for g in range(16):
                for u in range(2):
                    w = 2 * pair + u
                    tiles[at + 16 * half + g, 16 * w:16 * (w + 1), :] = (
                        got[16 * g:16 * (g + 1), u * LANES:(u + 1) * LANES]
                    )


def transposed_tiles(hats, flipped):
    r = lax.broadcasted_iota(jnp.int32, (BLOCK, LANES), 0)
    c = lax.broadcasted_iota(jnp.int32, (BLOCK, LANES), 1)
    pick = (c == 2 * (r % 32) + r // 32).astype(BF16)
    left = left_side(BLOCK)

    def body(p, carry):
        for inner in range(4):
            g = 8 * p + 2 * inner
            one, two = hats[g], hats[g + 1]
            stacked = jnp.concatenate([one, rotate(one), two, rotate(two)], axis=0)
            both = lax.dot_general(
                pick, stacked, (((1,), (1,)), ((), ())), preferred_element_type=F32
            ).astype(BF16)
            turned = rotate(both)
            flipped[g] = jnp.where(left, both, turned)
            flipped[g + 1] = jnp.where(left, turned, both)
        return carry

    lax.fori_loop(0, 4, body, 0)


def pair_flipped(p, order, flipped):
    return jnp.where(left_side(BLOCK), flipped[order[2 * p]], flipped[order[2 * p + 1]])


def pair_products(p, k, first, order, cols, blocks, tiles):
    left, wide = left_side(32), left_side(BLOCK)
    g1, g2 = order[2 * p], order[2 * p + 1]
    a1 = blocks[k * ROWS + g1]
    a2 = blocks[k * ROWS + g2]
    even = jnp.where(left, a1, rotate(a2))
    odd = jnp.where(left, rotate(a1), a2)
    lhs = jnp.concatenate([even, odd], axis=0)
    nil = jnp.zeros((BLOCK, LANES), BF16)
    p1 = tiles[jnp.clip(cols[k, g1] - first, 0, 3 * ROWS - 1)]
    p2 = tiles[jnp.clip(cols[k, g2] - first, 0, 3 * ROWS - 1)]
    rhs = jnp.concatenate([jnp.where(wide, p1, nil), jnp.where(wide, nil, p2)], axis=0)
    return dot(lhs, rhs).astype(BF16)


def pair_terms(outer, product):
    wide = left_side(BLOCK)
    nil = jnp.zeros((BLOCK, LANES), BF16)
    spread = jnp.concatenate(
        [jnp.where(wide, product, nil), jnp.where(wide, nil, product)], axis=0
    )
    return dot(outer, spread)


def split_pair(total):
    left = left_side(32)
    even, odd = total[:32], total[32:]
    return jnp.where(left, even, rotate(odd)), jnp.where(left, rotate(even), odd)


def invert_all(v):
    lanes = lax.broadcasted_iota(jnp.int32, (BLOCK, LANES), 1)
    sub = lax.broadcasted_iota(jnp.int32, (8, LANES), 0)
    slab_of = lambda k: 2 * (k // 16) + k % 2
    for k in range(BLOCK):
        q, sk, nxt = (k // 2) % 8, slab_of(k), slab_of(min(k + 1, BLOCK - 1))
        near = (k // 8) * 8
        index = (lanes // 8) * 8 + q
        row = jnp.take_along_axis(v[pl.ds(sk * BLOCK, BLOCK), :], index, axis=1)
        inverse = 1.0 / row[k:k + 1]
        scaled = row * inverse
        here = sub == k - near
        picked = lanes[:8] % 8 == q
        inverse = jnp.broadcast_to(inverse, (8, LANES))
        for s in [nxt] + [s for s in range(8) if s != nxt]:
            col = jnp.broadcast_to(v[pl.ds(s * BLOCK + k, 1), :], (8, LANES))
            for j in [near] + [j for j in range(0, BLOCK, 8) if j != near]:
                old = v[pl.ds(s * BLOCK + j, 8), :]
                part = scaled[j:j + 8]
                if j == near:
                    old = jnp.where(here, 0.0, old)
                    part = jnp.where(here, inverse, part)
                new = old - col * part
                if s == sk:
                    new = jnp.where(picked, part, new)
                v[pl.ds(s * BLOCK + j, 8), :] = new


def kernel(
    order, cols, a_hbm, p_hbm, coarse_ref, inverse_ref,
    a_flat, p_flat, halo, blocks, hats, tiles, flipped, swap, products,
    first_send, first_got, rest_send, rest_got, kept, whole, nat, v,
    a_sem, p_sem, halo_send, halo_recv, first_sem, rest_send_sem, rest_recv_sem,
):
    slab = lax.axis_index("slab")
    mirror = lax.axis_index("mirror")
    mirrors = lax.axis_size("mirror")
    partner = slab + 1 - 2 * (slab % 2)
    up = (mirror + 1) % mirrors
    down = (mirror + mirrors - 1) % mirrors
    others = ({"mirror": up}, {"mirror": down}, {"slab": partner})
    first_row = (slab * mirrors + mirror - 1) * ROWS

    own = pltpu.make_async_copy(p_hbm, p_flat, p_sem)
    own.start()
    loads = [
        pltpu.make_async_copy(a_hbm.at[k], a_flat.at[k], a_sem.at[k]) for k in range(KA)
    ]
    for load in loads:
        load.start()

    barrier = pltpu.get_barrier_semaphore()
    for other in others:
        pl.semaphore_signal(barrier, inc=1, device_id=other, device_id_type=MESH)
    swap_matrix(swap)
    pl.semaphore_wait(barrier, 3)

    halos = [
        pltpu.make_async_remote_copy(
            src_ref=p_hbm, dst_ref=halo.at[side], send_sem=halo_send.at[side],
            recv_sem=halo_recv.at[side], device_id=target, device_id_type=MESH,
        )
        for side, target in enumerate(({"mirror": up}, {"mirror": down}))
    ]
    for copy in halos:
        copy.start()

    def cut(half, t):
        return slice(16 * half, 16 * half + 16), slice(t * LANES, (t + 1) * LANES)

    own.wait()
    blocks_from_rows(lambda half, t: p_flat[cut(half, t)], hats, 0, swap)
    tiles_from_rows(lambda half, t: p_flat[cut(half, t)], tiles, ROWS, swap)
    loads[0].wait()
    blocks_from_rows(lambda half, t: a_flat[(0, *cut(half, t))], blocks, 0, swap)
    transposed_tiles(hats, flipped)

    args = (first_row, order, cols, blocks, tiles)

    def first_terms(p):
        return pair_terms(pair_flipped(p, order, flipped), pair_products(p, 0, *args))

    for p in range(PAIRS):
        first_send[p * BLOCK:(p + 1) * BLOCK, :] = first_terms(p).astype(BF16)
    first = pltpu.make_async_remote_copy(
        src_ref=first_send, dst_ref=first_got, send_sem=first_sem.at[0],
        recv_sem=first_sem.at[1], device_id={"slab": partner}, device_id_type=MESH,
    )
    first.start()
    for p in range(PAIRS):
        kept[p * BLOCK:(p + 1) * BLOCK, :] = first_terms(p + PAIRS)

    for k in range(1, KA):
        loads[k].wait()

    def rest_blocks(k, carry):
        blocks_from_rows(lambda half, t: a_flat[(k, *cut(half, t))], blocks, k * ROWS, swap)
        return carry

    lax.fori_loop(1, KA, rest_blocks, 0)

    first.wait()

    wide = left_side(BLOCK)

    def diagonal(i, carry):
        for inner in range(4):
            p = 4 * i + inner
            total = kept[rows_of(p, BLOCK), :] + first_got[rows_of(p, BLOCK), :].astype(F32)
            one, two = split_pair(total.astype(BF16))
            whole[2 * p] = one
            whole[2 * p + 1] = two
            at = pl.multiple_of(p * BLOCK, BLOCK)
            nat[pl.ds(at, 32, stride=2), :] = total[:32]
            nat[pl.ds(at + 1, 32, stride=2), :] = total[32:]
            plain = nat[rows_of(p, BLOCK), :]
            turned = jnp.concatenate([plain, plain], axis=0).T
            turned = jnp.where(wide, turned[:BLOCK], turned[BLOCK:])
            nat[rows_of(p, BLOCK), :] = 0.5 * (plain + turned)
            even = nat[pl.ds(at, 32, stride=2), :]
            odd = nat[pl.ds(at + 1, 32, stride=2), :]
            one, two = split_pair(jnp.concatenate([even, odd], axis=0))
            kept[rows_of(2 * p, TILES), :] = one
            kept[rows_of(2 * p + 1, TILES), :] = two
        return carry

    lax.fori_loop(0, PAIRS // 4, diagonal, 0)
    for tk in range(4):
        stacked = jnp.concatenate(
            [kept[pl.ds(b * TILES + tk * 8, 8), :] for b in range(HALF)], axis=0
        )
        v[pl.ds(tk * LANES, LANES), :] = stacked.T
    invert_all(v)
    for tk in range(4):
        stacked = v[pl.ds(tk * LANES, LANES), :].T
        for b in range(HALF):
            nat[pl.ds(b * TILES + tk * 8, 8), :] = stacked[b * 8:(b + 1) * 8]
    for t in range(TILES):
        inverse_ref[:, t * LANES:(t + 1) * LANES] = nat[pl.ds(t, HALF, stride=TILES), :]

    for side in range(2):
        halos[side].wait()

    def halo_tiles(side, carry):
        tiles_from_rows(
            lambda half, t: halo[(side, *cut(half, t))], tiles, 2 * ROWS * side, swap
        )
        return carry

    lax.fori_loop(0, 2, halo_tiles, 0)

    per = PAIRS // CHUNKS
    rest = KA - 1

    def multiply(p):
        for k in range(1, KA):
            products[k - 1] = pair_products(p, k, *args)

    def project(p, put):
        outer = pair_flipped(p, order, flipped)
        for k in range(1, KA):
            put(k - 1, pair_terms(outer, products[k - 1]))

    def put_out(p, k, term):
        rest_send[p // per, rows_of((p % per) * rest + k, BLOCK), :] = term.astype(BF16)

    def put_kept(p, k, term):
        kept[rows_of(p * rest + k, BLOCK), :] = term

    multiply(0)
    sends = []
    for chunk in range(CHUNKS):
        def rest_out(p, carry):
            project(p, lambda k, term: put_out(p, k, term))
            multiply(p + 1)
            return carry

        lax.fori_loop(chunk * per, (chunk + 1) * per, rest_out, 0)
        copy = pltpu.make_async_remote_copy(
            src_ref=rest_send.at[chunk], dst_ref=rest_got.at[chunk],
            send_sem=rest_send_sem.at[chunk], recv_sem=rest_recv_sem.at[chunk],
            device_id={"slab": partner}, device_id_type=MESH,
        )
        copy.start()
        sends.append(copy)

    def rest_kept(p, carry):
        project(p + PAIRS, lambda k, term: put_kept(p, k, term))
        multiply(p + PAIRS + 1)
        return carry

    lax.fori_loop(0, PAIRS - 1, rest_kept, 0)
    project(HALF - 1, lambda k, term: put_kept(PAIRS - 1, k, term))
    for chunk in range(CHUNKS):
        sends[chunk].wait()

        def add(p, carry):
            for k in range(1, KA):
                got = rest_got[p // per, rows_of((p % per) * rest + k - 1, BLOCK), :]
                total = kept[rows_of(p * rest + k - 1, BLOCK), :] + got.astype(F32)
                one, two = split_pair(total.astype(BF16))
                whole[k * HALF + 2 * p] = one
                whole[k * HALF + 2 * p + 1] = two
            return carry

        lax.fori_loop(chunk * per, (chunk + 1) * per, add, 0)

    def flatten(k, carry):
        got = swapped(
            swap,
            [[whole[k * HALF + c, 16 * u:16 * (u + 1), :] for c in range(HALF)] for u in range(2)],
        )
        for u in range(2):
            for t in range(16):
                at = (16 * u + t) * LANES
                coarse_ref[k, :, at:at + LANES] = (
                    got[16 * t:16 * (t + 1), u * LANES:(u + 1) * LANES]
                )
        return carry

    lax.fori_loop(0, KA, flatten, 0)


def on_device(a_blocks, a_cols, p_blocks, p_agg):
    mirrors = lax.axis_size("mirror")
    slab = lax.axis_index("slab")
    mine = ((p_agg // HALF) // mirrors) % 2 == slab % 2
    place = p_agg % HALF + HALF * mine.astype(jnp.int32)
    row = jnp.arange(ROWS, dtype=jnp.int32)
    order = jnp.sum(jnp.where(place[None, :] == row[:, None], row[None, :], 0), axis=1)

    vmem = lambda *shape: pltpu.VMEM(shape, F32)
    half = lambda *shape: pltpu.VMEM(shape, BF16)
    dma = pltpu.SemaphoreType.DMA
    coarse, inverse = pl.pallas_call(
        kernel,
        out_shape=(
            jax.ShapeDtypeStruct((KA, HALF, BLOCK * BLOCK), BF16),
            jax.ShapeDtypeStruct((HALF, BLOCK * BLOCK), F32),
        ),
        in_specs=[
            pl.BlockSpec(memory_space=pltpu.SMEM),
            pl.BlockSpec(memory_space=pltpu.SMEM),
            pl.BlockSpec(memory_space=pl.ANY),
            pl.BlockSpec(memory_space=pl.ANY),
        ],
        out_specs=(
            pl.BlockSpec(memory_space=pltpu.VMEM),
            pl.BlockSpec(memory_space=pltpu.VMEM),
        ),
        scratch_shapes=[
            half(KA, ROWS, BLOCK * BLOCK),
            half(ROWS, BLOCK * BLOCK),
            half(2, ROWS, BLOCK * BLOCK),
            half(KA * ROWS, TILES, LANES),
            half(ROWS, TILES, LANES),
            half(3 * ROWS, BLOCK, LANES),
            half(ROWS, BLOCK, LANES),
            half(256, 256),
            half(KA - 1, BLOCK, LANES),
            half(PAIRS * BLOCK, LANES),
            half(PAIRS * BLOCK, LANES),
            half(CHUNKS, PAIRS // CHUNKS * (KA - 1) * BLOCK, LANES),
            half(CHUNKS, PAIRS // CHUNKS * (KA - 1) * BLOCK, LANES),
            vmem(PAIRS * (KA - 1) * BLOCK, LANES),
            half(KA * HALF, TILES, LANES),
            vmem(PAIRS * BLOCK, LANES),
            vmem(4 * LANES, LANES),
            dma((KA,)), dma, dma((2,)), dma((2,)), dma((2,)), dma((CHUNKS,)), dma((CHUNKS,)),
        ],
        compiler_params=pltpu.CompilerParams(
            collective_id=0, has_side_effects=True, vmem_limit_bytes=56 * 2**20
        ),
    )(order, jnp.transpose(a_cols), jnp.transpose(a_blocks, (1, 0, 2)), p_blocks)
    return jnp.transpose(coarse, (1, 0, 2)), inverse


def solution(mesh):
    placed = (
        P(("slab", "mirror"), None, None),
        P(("slab", "mirror"), None),
        P(("slab", "mirror"), None),
        P(("slab", "mirror")),
    )
    return jax.shard_map(
        on_device,
        mesh=mesh,
        in_specs=placed,
        out_specs=(P(("slab", "mirror"), None, None), P(("slab", "mirror"), None)),
        check_vma=False,
    )
```

```python
import functools

import jax
import jax.numpy as jnp
from jax import lax
from jax.experimental import pallas as pl
from jax.experimental.pallas import tpu as pltpu
from jax.sharding import PartitionSpec as P

F32, BF16 = jnp.float32, jnp.bfloat16
BLOCK = 64
LANES = 128
ROWS = 32
HALF = ROWS // 2
PAIRS = HALF // 2
KA = 7
TILES = BLOCK * BLOCK // LANES
CHUNKS = 4
MESH = pl.DeviceIdType.MESH


def rotate(value):
    return pltpu.roll(value, BLOCK, 1)


def dot(left, right):
    return lax.dot_general(left, right, (((1,), (0,)), ((), ())), preferred_element_type=F32)


def rows_of(index, count):
    return pl.ds(pl.multiple_of(index * count, count), count)


def left_side(rows):
    return lax.broadcasted_iota(jnp.int32, (rows, LANES), 1) < BLOCK


def swap_matrix(swap):
    r = lax.broadcasted_iota(jnp.int32, (256, 256), 0)
    c = lax.broadcasted_iota(jnp.int32, (256, 256), 1)
    swap[...] = (c == (r % 16) * 16 + r // 16).astype(BF16)


def swapped(swap, parts):
    stacked = [jnp.concatenate(part, axis=0) for part in parts]
    return dot(swap[...], jnp.concatenate(stacked, axis=1)).astype(BF16)


def blocks_from_rows(tile, blocks, at, swap):
    for half in range(2):
        got = swapped(
            swap, [[tile(half, 16 * u + t) for t in range(16)] for u in range(2)]
        )
        for g in range(16):
            for u in range(2):
                blocks[at + 16 * half + g, 16 * u:16 * (u + 1), :] = (
                    got[16 * g:16 * (g + 1), u * LANES:(u + 1) * LANES]
                )


def tiles_from_rows(tile, tiles, at, swap):
    left = left_side(16)
    for half in range(2):
        for pair in range(2):
            parts = []
            for w in (2 * pair, 2 * pair + 1):
                part = []
                for t in range(8 * w, 8 * w + 8):
                    plain = tile(half, t)
                    turned = rotate(plain)
                    part += [jnp.where(left, plain, turned), jnp.where(left, turned, plain)]
                parts.append(part)
            got = swapped(swap, parts)
            for g in range(16):
                for u in range(2):
                    w = 2 * pair + u
                    tiles[at + 16 * half + g, 16 * w:16 * (w + 1), :] = (
                        got[16 * g:16 * (g + 1), u * LANES:(u + 1) * LANES]
                    )


def transposed_tiles(hats, flipped):
    r = lax.broadcasted_iota(jnp.int32, (BLOCK, LANES), 0)
    c = lax.broadcasted_iota(jnp.int32, (BLOCK, LANES), 1)
    pick = (c == 2 * (r % 32) + r // 32).astype(BF16)
    left = left_side(BLOCK)

    def body(p, carry):
        for inner in range(4):
            g = 8 * p + 2 * inner
            one, two = hats[g], hats[g + 1]
            stacked = jnp.concatenate([one, rotate(one), two, rotate(two)], axis=0)
            both = lax.dot_general(
                pick, stacked, (((1,), (1,)), ((), ())), preferred_element_type=F32
            ).astype(BF16)
            turned = rotate(both)
            flipped[g] = jnp.where(left, both, turned)
            flipped[g + 1] = jnp.where(left, turned, both)
        return carry

    lax.fori_loop(0, 4, body, 0)


def pair_flipped(p, order, flipped):
    return jnp.where(left_side(BLOCK), flipped[order[2 * p]], flipped[order[2 * p + 1]])


def pair_products(p, k, first, order, cols, blocks, tiles):
    left, wide = left_side(32), left_side(BLOCK)
    g1, g2 = order[2 * p], order[2 * p + 1]
    a1 = blocks[k * ROWS + g1]
    a2 = blocks[k * ROWS + g2]
    even = jnp.where(left, a1, rotate(a2))
    odd = jnp.where(left, rotate(a1), a2)
    lhs = jnp.concatenate([even, odd], axis=0)
    nil = jnp.zeros((BLOCK, LANES), BF16)
    p1 = tiles[jnp.clip(cols[k, g1] - first, 0, 3 * ROWS - 1)]
    p2 = tiles[jnp.clip(cols[k, g2] - first, 0, 3 * ROWS - 1)]
    rhs = jnp.concatenate([jnp.where(wide, p1, nil), jnp.where(wide, nil, p2)], axis=0)
    return dot(lhs, rhs).astype(BF16)


def pair_terms(outer, product):
    wide = left_side(BLOCK)
    nil = jnp.zeros((BLOCK, LANES), BF16)
    spread = jnp.concatenate(
        [jnp.where(wide, product, nil), jnp.where(wide, nil, product)], axis=0
    )
    return dot(outer, spread)


def split_pair(total):
    left = left_side(32)
    even, odd = total[:32], total[32:]
    return jnp.where(left, even, rotate(odd)), jnp.where(left, rotate(even), odd)


def invert_all(v, meanwhile):
    lanes = lax.broadcasted_iota(jnp.int32, (BLOCK, LANES), 1)
    sub = lax.broadcasted_iota(jnp.int32, (8, LANES), 0)
    slab_of = lambda k: 2 * (k // 16) + k % 2
    for k in range(BLOCK):
        if k in meanwhile:
            meanwhile[k]()
        q, sk, nxt = (k // 2) % 8, slab_of(k), slab_of(min(k + 1, BLOCK - 1))
        near = (k // 8) * 8
        index = (lanes // 8) * 8 + q
        row = jnp.take_along_axis(v[pl.ds(sk * BLOCK, BLOCK), :], index, axis=1)
        inverse = 1.0 / row[k:k + 1]
        scaled = row * inverse
        here = sub == k - near
        picked = lanes[:8] % 8 == q
        inverse = jnp.broadcast_to(inverse, (8, LANES))
        for s in [nxt] + [s for s in range(8) if s != nxt]:
            col = jnp.broadcast_to(v[pl.ds(s * BLOCK + k, 1), :], (8, LANES))
            for j in [near] + [j for j in range(0, BLOCK, 8) if j != near]:
                old = v[pl.ds(s * BLOCK + j, 8), :]
                part = scaled[j:j + 8]
                if j == near:
                    old = jnp.where(here, 0.0, old)
                    part = jnp.where(here, inverse, part)
                new = old - col * part
                if s == sk:
                    new = jnp.where(picked, part, new)
                v[pl.ds(s * BLOCK + j, 8), :] = new


def kernel(
    order, cols_hbm, a_hbm, p_hbm, coarse_ref, inverse_ref,
    cols, a_flat, p_flat, halo, blocks, hats, tiles, flipped, swap, products,
    first_send, first_got, rest_send, rest_got, kept, whole, nat, v,
    cols_sem, a_sem, p_sem, halo_send, halo_recv, first_sem, rest_send_sem, rest_recv_sem,
):
    slab = lax.axis_index("slab")
    mirror = lax.axis_index("mirror")
    mirrors = lax.axis_size("mirror")
    partner = slab + 1 - 2 * (slab % 2)
    up = (mirror + 1) % mirrors
    down = (mirror + mirrors - 1) % mirrors
    others = ({"mirror": up}, {"mirror": down}, {"slab": partner})
    first_row = (slab * mirrors + mirror - 1) * ROWS

    own = pltpu.make_async_copy(p_hbm, p_flat, p_sem)
    own.start()
    index = pltpu.make_async_copy(cols_hbm, cols, cols_sem)
    index.start()
    loads = [
        pltpu.make_async_copy(a_hbm.at[k], a_flat.at[k], a_sem.at[k]) for k in range(KA)
    ]
    for load in loads:
        load.start()

    barrier = pltpu.get_barrier_semaphore()
    for other in others:
        pl.semaphore_signal(barrier, inc=1, device_id=other, device_id_type=MESH)
    swap_matrix(swap)
    pl.semaphore_wait(barrier, 3)

    halos = [
        pltpu.make_async_remote_copy(
            src_ref=p_hbm, dst_ref=halo.at[side], send_sem=halo_send.at[side],
            recv_sem=halo_recv.at[side], device_id=target, device_id_type=MESH,
        )
        for side, target in enumerate(({"mirror": up}, {"mirror": down}))
    ]
    for copy in halos:
        copy.start()

    def cut(half, t):
        return slice(16 * half, 16 * half + 16), slice(t * LANES, (t + 1) * LANES)

    own.wait()
    blocks_from_rows(lambda half, t: p_flat[cut(half, t)], hats, 0, swap)
    tiles_from_rows(lambda half, t: p_flat[cut(half, t)], tiles, ROWS, swap)
    loads[0].wait()
    blocks_from_rows(lambda half, t: a_flat[(0, *cut(half, t))], blocks, 0, swap)
    transposed_tiles(hats, flipped)
    index.wait()

    args = (first_row, order, cols, blocks, tiles)

    def first_terms(p):
        return pair_terms(pair_flipped(p, order, flipped), pair_products(p, 0, *args))

    for p in range(PAIRS):
        first_send[p * BLOCK:(p + 1) * BLOCK, :] = first_terms(p).astype(BF16)
    first = pltpu.make_async_remote_copy(
        src_ref=first_send, dst_ref=first_got, send_sem=first_sem.at[0],
        recv_sem=first_sem.at[1], device_id={"slab": partner}, device_id_type=MESH,
    )
    first.start()
    for p in range(PAIRS):
        kept[p * BLOCK:(p + 1) * BLOCK, :] = first_terms(p + PAIRS)

    for k in range(1, KA):
        loads[k].wait()

    def rest_blocks(k):
        blocks_from_rows(lambda half, t: a_flat[(k, *cut(half, t))], blocks, k * ROWS, swap)

    for k in range(1, 4):
        rest_blocks(k)
    first.wait()

    wide = left_side(BLOCK)

    def diagonal(i, carry):
        for inner in range(4):
            p = 4 * i + inner
            total = kept[rows_of(p, BLOCK), :] + first_got[rows_of(p, BLOCK), :].astype(F32)
            one, two = split_pair(total.astype(BF16))
            whole[2 * p] = one
            whole[2 * p + 1] = two
            at = pl.multiple_of(p * BLOCK, BLOCK)
            nat[pl.ds(at, 32, stride=2), :] = total[:32]
            nat[pl.ds(at + 1, 32, stride=2), :] = total[32:]
            plain = nat[rows_of(p, BLOCK), :]
            turned = jnp.concatenate([plain, plain], axis=0).T
            turned = jnp.where(wide, turned[:BLOCK], turned[BLOCK:])
            nat[rows_of(p, BLOCK), :] = 0.5 * (plain + turned)
            even = nat[pl.ds(at, 32, stride=2), :]
            odd = nat[pl.ds(at + 1, 32, stride=2), :]
            one, two = split_pair(jnp.concatenate([even, odd], axis=0))
            kept[rows_of(2 * p, TILES), :] = one
            kept[rows_of(2 * p + 1, TILES), :] = two
        return carry

    lax.fori_loop(0, PAIRS // 4, diagonal, 0)
    for tk in range(4):
        stacked = jnp.concatenate(
            [kept[pl.ds(b * TILES + tk * 8, 8), :] for b in range(HALF)], axis=0
        )
        v[pl.ds(tk * LANES, LANES), :] = stacked.T

    def halo_tiles(side):
        halos[side].wait()
        tiles_from_rows(
            lambda half, t: halo[(side, *cut(half, t))], tiles, 2 * ROWS * side, swap
        )

    meanwhile = {10 * k - 38: functools.partial(rest_blocks, k) for k in range(4, KA)}
    meanwhile[38] = functools.partial(halo_tiles, 0)
    meanwhile[50] = functools.partial(halo_tiles, 1)
    invert_all(v, meanwhile)
    for tk in range(4):
        stacked = v[pl.ds(tk * LANES, LANES), :].T
        for b in range(HALF):
            nat[pl.ds(b * TILES + tk * 8, 8), :] = stacked[b * 8:(b + 1) * 8]
    for t in range(TILES):
        inverse_ref[:, t * LANES:(t + 1) * LANES] = nat[pl.ds(t, HALF, stride=TILES), :]

    per = PAIRS // CHUNKS
    rest = KA - 1

    def multiply(p, side):
        for k in range(1, KA):
            products[side * rest + k - 1] = pair_products(p, k, *args)

    def project(p, side, put):
        outer = pair_flipped(p, order, flipped)
        for k in range(rest):
            put(k, pair_terms(outer, products[side * rest + k]))

    def put_kept(p, k, term):
        kept[rows_of(p * rest + k, BLOCK), :] = term

    for side in range(per):
        multiply(side, side)
    sends = []
    for chunk in range(CHUNKS):
        for side in range(per):
            def put_out(k, term):
                at = (side * rest + k) * BLOCK
                rest_send[chunk, at:at + BLOCK, :] = term.astype(BF16)

            project(chunk * per + side, side, put_out)
        for side in range(per):
            multiply((chunk + 1) * per + side, side)
        copy = pltpu.make_async_remote_copy(
            src_ref=rest_send.at[chunk], dst_ref=rest_got.at[chunk],
            send_sem=rest_send_sem.at[chunk], recv_sem=rest_recv_sem.at[chunk],
            device_id={"slab": partner}, device_id_type=MESH,
        )
        copy.start()
        sends.append(copy)

    def rest_kept(i, carry):
        for side in range(per):
            p = i * per + side
            project(p + PAIRS, side, functools.partial(put_kept, p))
        for side in range(per):
            multiply((i + 1) * per + side + PAIRS, side)
        return carry

    lax.fori_loop(0, CHUNKS - 1, rest_kept, 0)
    for side in range(per):
        p = PAIRS - per + side
        project(p + PAIRS, side, functools.partial(put_kept, p))
    for chunk in range(CHUNKS):
        sends[chunk].wait()

        def add(p, carry):
            for k in range(1, KA):
                got = rest_got[p // per, rows_of((p % per) * rest + k - 1, BLOCK), :]
                total = kept[rows_of(p * rest + k - 1, BLOCK), :] + got.astype(F32)
                one, two = split_pair(total.astype(BF16))
                whole[k * HALF + 2 * p] = one
                whole[k * HALF + 2 * p + 1] = two
            return carry

        lax.fori_loop(chunk * per, (chunk + 1) * per, add, 0)

    for k in range(KA):
        got = swapped(
            swap,
            [[whole[k * HALF + c, 16 * u:16 * (u + 1), :] for c in range(HALF)] for u in range(2)],
        )
        for u in range(2):
            for t in range(16):
                at = (16 * u + t) * LANES
                coarse_ref[k, :, at:at + LANES] = (
                    got[16 * t:16 * (t + 1), u * LANES:(u + 1) * LANES]
                )


def on_device(a_blocks, a_cols, p_blocks, p_agg):
    mirrors = lax.axis_size("mirror")
    slab = lax.axis_index("slab")
    row = jnp.arange(ROWS, dtype=jnp.int32)
    device = slab * mirrors + lax.axis_index("mirror")
    partner = (slab + 1 - 2 * (slab % 2)) * mirrors + lax.axis_index("mirror")
    target = jnp.where(row < HALF, partner * HALF + row, device * HALF + row - HALF)
    order = jnp.sum(jnp.where(p_agg[None, :] == target[:, None], row[None, :], 0), axis=1)

    vmem = lambda *shape: pltpu.VMEM(shape, F32)
    half = lambda *shape: pltpu.VMEM(shape, BF16)
    dma = pltpu.SemaphoreType.DMA
    coarse, inverse = pl.pallas_call(
        kernel,
        out_shape=(
            jax.ShapeDtypeStruct((KA, HALF, BLOCK * BLOCK), BF16),
            jax.ShapeDtypeStruct((HALF, BLOCK * BLOCK), F32),
        ),
        in_specs=[
            pl.BlockSpec(memory_space=pltpu.SMEM),
            pl.BlockSpec(memory_space=pltpu.HBM),
            pl.BlockSpec(memory_space=pltpu.HBM),
            pl.BlockSpec(memory_space=pltpu.HBM),
        ],
        out_specs=(
            pl.BlockSpec(memory_space=pltpu.VMEM),
            pl.BlockSpec(memory_space=pltpu.VMEM),
        ),
        scratch_shapes=[
            pltpu.SMEM((KA, ROWS), jnp.int32),
            half(KA, ROWS, BLOCK * BLOCK),
            half(ROWS, BLOCK * BLOCK),
            half(2, ROWS, BLOCK * BLOCK),
            half(KA * ROWS, TILES, LANES),
            half(ROWS, TILES, LANES),
            half(3 * ROWS, BLOCK, LANES),
            half(ROWS, BLOCK, LANES),
            half(256, 256),
            half(PAIRS // CHUNKS * (KA - 1), BLOCK, LANES),
            half(PAIRS * BLOCK, LANES),
            half(PAIRS * BLOCK, LANES),
            half(CHUNKS, PAIRS // CHUNKS * (KA - 1) * BLOCK, LANES),
            half(CHUNKS, PAIRS // CHUNKS * (KA - 1) * BLOCK, LANES),
            vmem(PAIRS * (KA - 1) * BLOCK, LANES),
            half(KA * HALF, TILES, LANES),
            vmem(PAIRS * BLOCK, LANES),
            vmem(4 * LANES, LANES),
            dma, dma((KA,)), dma, dma((2,)), dma((2,)), dma((2,)), dma((CHUNKS,)), dma((CHUNKS,)),
        ],
        compiler_params=pltpu.CompilerParams(
            collective_id=0, has_side_effects=True, vmem_limit_bytes=51 * 2**20
        ),
    )(order, jnp.transpose(a_cols), jnp.transpose(a_blocks, (1, 0, 2)), p_blocks)
    return jnp.transpose(coarse, (1, 0, 2)), inverse


def solution(mesh):
    placed = (
        P(("slab", "mirror"), None, None),
        P(("slab", "mirror"), None),
        P(("slab", "mirror"), None),
        P(("slab", "mirror")),
    )
    return jax.shard_map(
        on_device,
        mesh=mesh,
        in_specs=placed,
        out_specs=(P(("slab", "mirror"), None, None), P(("slab", "mirror"), None)),
        check_vma=False,
    )
```
